32 devices in a mesh: gx: 2 (over x), gy: 4 (over y, core), gz: 4 (over z).
Axes of the slice: x: 2, y: 2, z: 4, core: 2. Of those that a mesh axis runs over, the one named last changes fastest.
Arguments:
- solution_in: float32 [16, 128, 512], P('gx', 'gy', 'gz'), may hold values from -6 to 6
- residual_in: float32 [16, 128, 512], P('gx', 'gy', 'gz'), may hold values from -12 to 12
- direction_in: float32 [16, 128, 512], P('gx', 'gy', 'gz'), may hold values from -6 to 6
- material: int32 [16, 128, 512], P('gx', 'gy', 'gz'), may hold values from 0 to 7
- cond_table: float32 [8], replicated, may hold values from 0.5 to 4
- cap_table: float32 [8], replicated, may hold values from 0.2 to 1
- gas_flux: float32 [128, 512], P('gy', 'gz'), may hold values from -6 to 6
- supply_map: int32 [128, 512], P('gy', 'gz'), may hold values from 0 to 511, as said below
Outputs:
- solution: float32 [16, 128, 512], P('gx', 'gy', 'gz')
- residual: float32 [16, 128, 512], P('gx', 'gy', 'gz')
- direction: float32 [16, 128, 512], P('gx', 'gy', 'gz')
The draws below stay inside these ranges and needn't reach their ends.
Inputs may be any that keep to these rules, and one draw needn't show every extreme that they name: `supply_map`: the gas faces are laid out so that the faces held by index q of gz, in their slots t * 128 / 4 to (t + 1) * 128 / 4 - 1, supply solid faces held by index t of gz in the same row; every gas face supplies exactly one solid face of its row.
All inputs are finite; a program needn't handle non-finite values.
Results may differ from the reference program's by a relative error of at most 0.0006.
Values sent between devices are 32-bit elements; how exact they have to be, the bound alone decides.
A program may use at most 64 MiB of HBM per device.

```python
import math
import jax
import jax.numpy as jnp
from jax import lax

CZ = 128
STEPS = 4
MATERIALS = 8
NX = 16
NY = 128
NZ = 512


def draw_residual_in(key, part):
    depth = jnp.arange(NX, dtype=jnp.float32) / NX
    scaling = (0.5 + 1.5 * depth)[:, None, None]
    base = jax.random.truncated_normal(key, -6.0, 6.0, (NX, NY, NZ), jnp.float32)
    return base * scaling


def draw_supply_map(key, part):
    groups = NZ // CZ
    segment = CZ // groups
    keys = jax.random.split(jax.random.fold_in(key, 7), NY * groups)
    orders = jax.vmap(lambda single: jax.random.permutation(single, CZ))(keys).astype(jnp.int32)
    orders = orders.reshape(NY, groups, CZ)
    target = jnp.arange(groups, dtype=jnp.int32)[None, :, None]
    mapped = orders // segment * CZ + target * segment + orders % segment
    return mapped.reshape(NY, NZ).astype(jnp.int32)


def touch_ends(array, rng, low, high):
    longest = array.shape.index(max(array.shape))
    spots = []
    for shift in (0, 1):
        where = [jax.random.randint(jax.random.fold_in(rng, axis), (), 0, length) for axis, length in enumerate(array.shape)]
        where[longest] = (where[longest] + shift) % array.shape[longest]
        spots.append(tuple(where))
    return array.at[spots[0]].set(low).at[spots[1]].set(high)


def block_levels(stream_key, dims, pieces, least, high):
    level, own = 1.0, jax.random.fold_in(stream_key, 6)
    for dim, parts in pieces:
        steps = jnp.exp(jax.random.uniform(jax.random.fold_in(own, dim), (parts,), jnp.float32, least / len(pieces), high / len(pieces)))
        level = level * jnp.repeat(steps, dims[dim] // parts).reshape([-1 if axis == dim else 1 for axis in range(len(dims))])
    return level


def normal_values(stream_key, shape, scale, limit, cuts=(), kind=jnp.bfloat16):
    values = scale * jax.random.normal(stream_key, shape, jnp.float32)
    if cuts:
        values = values * block_levels(stream_key, shape, cuts, -0.22, 0.18)
    return jnp.clip(values, -limit, limit).astype(kind)


def setup_inputs(seed: int = 0) -> dict:
    arg_keys = jax.random.split(jax.random.key(seed), 9)
    solution_in = normal_values(arg_keys[0], (NX, NY, NZ), 1.0, 6.0, ((0, 2), (1, 4), (2, 4)), jnp.float32)
    residual_in = draw_residual_in(jax.random.fold_in(arg_keys[8], 71), 0)
    direction_in = normal_values(arg_keys[2], (NX, NY, NZ), 1.0, 6.0, ((0, 2), (1, 4), (2, 4)), jnp.float32)
    material = touch_ends(jax.random.randint(arg_keys[3], (NX, NY, NZ), 0, MATERIALS), jax.random.fold_in(arg_keys[3], 1), 0, MATERIALS - 1).astype(jnp.int32)
    cond_table = jnp.clip(jnp.exp(jax.random.uniform(arg_keys[4], (MATERIALS,), jnp.float32, math.log(0.5), math.log(4.0))), 0.5, 4.0)
    cap_table = jnp.clip(jnp.exp(jax.random.uniform(arg_keys[5], (MATERIALS,), jnp.float32, math.log(0.2), math.log(1.0))), 0.2, 1.0)
    gas_flux = normal_values(arg_keys[6], (NY, NZ), 1.0, 6.0, ((0, 4), (1, 4)), jnp.float32)
    supply_map = draw_supply_map(jax.random.fold_in(arg_keys[8], 71), 0)
    return dict(solution_in=solution_in, residual_in=residual_in, direction_in=direction_in, material=material, cond_table=cond_table, cap_table=cap_table, gas_flux=gas_flux, supply_map=supply_map)


def harmonic(lower_side, upper_side):
    return 2.0 * lower_side * upper_side / (jnp.where(lower_side > 0, lower_side, 1.0) + jnp.where(upper_side > 0, upper_side, 1.0))


def face_terms(cond):
    return (harmonic(cond[:-1], cond[1:]), harmonic(cond[:, :-1], cond[:, 1:]), harmonic(cond[:, :, :-1], cond[:, :, 1:]))


def operate(values, capacity, conductance):
    result = capacity * values
    face_flow = conductance[0] * (values[1:] - values[:-1])
    result = result - jnp.pad(face_flow, ((0, 1), (0, 0), (0, 0))) + jnp.pad(face_flow, ((1, 0), (0, 0), (0, 0)))
    face_flow = conductance[1] * (values[:, 1:] - values[:, :-1])
    result = result - jnp.pad(face_flow, ((0, 0), (0, 1), (0, 0))) + jnp.pad(face_flow, ((0, 0), (1, 0), (0, 0)))
    face_flow = conductance[2] * (values[:, :, 1:] - values[:, :, :-1])
    result = result - jnp.pad(face_flow, ((0, 0), (0, 0), (0, 1))) + jnp.pad(face_flow, ((0, 0), (0, 0), (1, 0)))
    return result


def lookup(material, table):
    summed = jnp.zeros(material.shape, jnp.float32)
    for material_id in range(table.shape[0]):
        summed = summed + jnp.where(material == material_id, table[material_id], jnp.float32(0.0))
    return summed


def spectrum(cond_table, cap_table):
    lowest = jnp.min(cap_table)
    highest = jnp.max(cap_table) + 12.0 * jnp.max(cond_table)
    return 0.5 * (highest + lowest), 0.5 * (highest - lowest)


def next_term(applied, terms, center, half_width):
    shifted = (applied - center * terms[-1]) / half_width
    if len(terms) == 1:
        return shifted
    return 2.0 * shifted - terms[-2]


def chebyshev(values, degree, capacity, conductance, center, half_width):
    terms = [values]
    for sweep in range(degree):
        terms.append(next_term(operate(terms[-1], capacity, conductance), terms, center, half_width))
    return terms


def shift_matrix(center, half_width, steps):
    dimension = 2 * steps + 1
    matrix = jnp.zeros((dimension, dimension), jnp.float32)
    for offset, length in ((0, steps + 1), (steps + 1, steps)):
        for column in range(length - 1):
            matrix = matrix.at[offset + column, offset + column].set(center)
            matrix = matrix.at[offset + column + 1, offset + column].set(half_width if column == 0 else 0.5 * half_width)
            if column >= 1:
                matrix = matrix.at[offset + column - 1, offset + column].set(0.5 * half_width)
    return matrix


def coefficients(gram, center, half_width, steps):
    dimension = 2 * steps + 1
    matrix = shift_matrix(center, half_width, steps)
    highest_prec = lax.Precision.HIGHEST

    def gram_product(first_vec, second_vec):
        return jnp.dot(first_vec, jnp.dot(gram, second_vec, precision=highest_prec), precision=highest_prec)

    direct = jnp.zeros((dimension,), jnp.float32).at[0].set(1.0)
    residue = jnp.zeros((dimension,), jnp.float32).at[steps + 1].set(1.0)
    moved = jnp.zeros((dimension,), jnp.float32)
    norm_now = gram_product(residue, residue)
    for sweep in range(steps):
        mapped = jnp.dot(matrix, direct, precision=highest_prec)
        step_length = norm_now / gram_product(direct, mapped)
        moved = moved + step_length * direct
        residue = residue - step_length * mapped
        norm_next = gram_product(residue, residue)
        direct = residue + (norm_next / norm_now) * direct
        norm_now = norm_next
    return moved, residue, direct


def combine(weights, basis):
    summed = weights[0] * basis[0]
    for position in range(1, len(basis)):
        summed = summed + weights[position] * basis[position]
    return summed


def reference(solution_in, residual_in, direction_in, material, cond_table, cap_table, gas_flux, supply_map):
    incoming = jnp.take_along_axis(gas_flux, supply_map, axis=1)
    start = residual_in.at[NX - 1].add(incoming)
    conductance = face_terms(lookup(material, cond_table))
    capacity = lookup(material, cap_table)
    center, half_width = spectrum(cond_table, cap_table)
    basis = chebyshev(direction_in, STEPS, capacity, conductance, center, half_width)
    basis = basis + chebyshev(start, STEPS - 1, capacity, conductance, center, half_width)
    dimension = len(basis)
    rows_list = []
    for first_id in range(dimension):
        entries = []
        for second_id in range(dimension):
            entries.append(jnp.sum(basis[first_id] * basis[second_id]))
        rows_list.append(jnp.stack(entries))
    gram = jnp.stack(rows_list)
    moved, residue, direct = coefficients(gram, center, half_width, STEPS)
    return (solution_in + combine(moved, basis), combine(residue, basis), combine(direct, basis))
```

```python
import jax
import jax.numpy as jnp
from jax import lax
from jax.experimental import pallas as pl
from jax.experimental.pallas import tpu as pltpu
from jax.sharding import PartitionSpec as P

STEPS = 4
AXES = ("gx", "gy", "gz")
MESH = pl.DeviceIdType.MESH
DIM = 2 * STEPS + 1
PAIRS = [(i, j) for i in range(DIM) for j in range(i, DIM)]
SLOT = {pair: k for k, pair in enumerate(PAIRS)}


def harmonic(a, b):
    return 2.0 * a * b / (a + b)


def times(a, b):
    return None if a is None or b is None else a * b


def plus(a, b):
    return b if a is None else a if b is None else a + b


def shift_product(p, center, half_width):
    q = [None] * DIM
    for offset, length in ((0, STEPS + 1), (STEPS + 1, STEPS)):
        for column in range(length - 1):
            entry = p[offset + column]
            if entry is None:
                continue
            q[offset + column] = plus(q[offset + column], center * entry)
            low = half_width if column == 0 else 0.5 * half_width
            q[offset + column + 1] = plus(q[offset + column + 1], low * entry)
            if column >= 1:
                q[offset + column - 1] = plus(q[offset + column - 1], 0.5 * half_width * entry)
    return q


def form(gram, a, b):
    total = None
    for i in range(DIM):
        if a[i] is None:
            continue
        row = None
        for j in range(DIM):
            row = plus(row, times(gram[i][j], b[j]))
        total = plus(total, a[i] * row)
    return total


def coefficients(gram, center, half_width):
    one = jnp.ones_like(gram[0][0])
    p = [None] * DIM
    r = [None] * DIM
    x = [None] * DIM
    p[0] = one
    r[STEPS + 1] = one
    rr = form(gram, r, r)
    for _ in range(STEPS):
        q = shift_product(p, center, half_width)
        step = rr / form(gram, p, q)
        x = [plus(x[i], times(step, p[i])) for i in range(DIM)]
        r = [plus(r[i], times(-step, q[i])) for i in range(DIM)]
        new = form(gram, r, r)
        ratio = new / rr
        p = [plus(r[i], times(ratio, p[i])) for i in range(DIM)]
        rr = new
    return x, r, p


def kernel(
    sizes, stages, cond_tab, cap_tab, sol_ref, res_ref, dir_ref, mat_ref, gas_ref, map_ref,
    sol_out, res_out, dir_out,
    basis, coef_x, coef_y, coef_z, edge_y, edge_z, diag, cond_ref,
    x_send, y_send, z_send, x_halo, y_halo, z_halo, flux_send, flux_halo, gram_send, gram_halo,
    send_sem, recv_sem, flux_ssem, flux_rsem, gram_ssem, gram_rsem,
):
    pos = {axis: lax.axis_index(axis) for axis in AXES}
    groups = sizes["gz"]
    segment = 128 // groups
    lane = lax.broadcasted_iota(jnp.int32, (8, 128), 1)
    sub = lax.broadcasted_iota(jnp.int32, (8, 128), 0)

    sides = []
    for number, axis in enumerate(AXES):
        if sizes[axis] > 1:
            sides.append((2 * number, axis, -1, pos[axis] > 0))
            sides.append((2 * number + 1, axis, 1, pos[axis] < sizes[axis] - 1))

    def zero(side):
        number, high = side // 2, side % 2
        ref = (x_halo, y_halo, z_halo)[number]
        ref[:, high] = jnp.zeros(ref.shape[:1] + ref.shape[2:], jnp.float32)

    for side in range(6):
        present = [entry[3] for entry in sides if entry[0] == side]
        if present:
            pl.when(jnp.logical_not(present[0]))(lambda side=side: zero(side))
        else:
            zero(side)

    def peers(axes):
        found = [{}]
        for axis in axes:
            found = [dict(entry, **{axis: o}) for entry in found for o in range(sizes[axis])]
        found = [entry for entry in found if any(entry.values())]
        return [
            {axis: lax.rem(pos[axis] + o, sizes[axis]) for axis, o in entry.items()} for entry in found
        ]

    def place(axes, where):
        index = 0
        for axis in axes:
            index = index * sizes[axis] + where[axis]
        return index

    barrier = pltpu.get_barrier_semaphore()
    count = 0
    for axes in stages:
        for peer in peers(axes):
            pl.semaphore_signal(barrier, inc=1, device_id=peer, device_id_type=MESH)
            count += 1

    material = mat_ref[...].reshape(32, 8, 128)
    cond = jnp.full((32, 8, 128), cond_tab[0], jnp.float32)
    cap = jnp.full((32, 8, 128), cap_tab[0], jnp.float32)
    cond_max = cond_tab[0]
    cap_max = cap_tab[0]
    cap_min = cap_tab[0]
    for m in range(1, 8):
        hit = material == m
        cond = jnp.where(hit, cond_tab[m], cond)
        cap = jnp.where(hit, cap_tab[m], cap)
        cond_max = jnp.maximum(cond_max, cond_tab[m])
        cap_max = jnp.maximum(cap_max, cap_tab[m])
        cap_min = jnp.minimum(cap_min, cap_tab[m])
    highest = cap_max + 12.0 * cond_max
    center = jnp.full((8, 128), 0.5 * (highest + cap_min), jnp.float32)
    half_width = jnp.full((8, 128), 0.5 * (highest - cap_min), jnp.float32)
    scale = 2.0 / half_width
    cond_ref[...] = cond.reshape(256, 128)

    odd = lax.rem(lane, 2) == 1
    pair_of = lax.rem(lane + 1, 128) // 2

    def copies(turn):
        result = []
        for side, axis, step, present in sides:
            number, high = side // 2, side % 2
            source = (x_send.at[turn, high], y_send.at[turn, high], z_send.at[turn])[number]
            target = (x_halo, y_halo, z_halo)[number].at[turn, 1 - high]
            result.append((side, present, pltpu.make_async_remote_copy(
                src_ref=source, dst_ref=target,
                send_sem=send_sem.at[turn, side], recv_sem=recv_sem.at[turn, side ^ 1],
                device_id={axis: pos[axis] + step}, device_id_type=MESH,
            )))
        return result

    def pack(turn, refs):
        tile = jnp.zeros((8, 128), jnp.float32)
        for f, ref in enumerate(refs):
            value = ref[...].reshape(32, 8, 128)
            x_send[turn, 0, f] = value[0:4]
            x_send[turn, 1, f] = value[28:32]
            y_send[turn, 0, f] = ref[pl.ds(0, 8, stride=32), :]
            y_send[turn, 1, f] = ref[pl.ds(31, 8, stride=32), :]
            for g in range(32):
                k = 32 * f + g
                moved = pltpu.roll(value[g], 2 * k, axis=1) if k else value[g]
                tile = jnp.where(pair_of == k, moved, tile)
        z_send[turn] = tile

    def start(turn):
        for side, present, copy in copies(turn):
            pl.when(present)(copy.start)

    def wait(turn):
        for side, axis, step, present in sides:
            number, high = side // 2, side % 2
            target = (x_halo, y_halo, z_halo)[number].at[turn, high]
            copy = pltpu.make_async_remote_copy(
                src_ref=target, dst_ref=target,
                send_sem=send_sem.at[turn, side], recv_sem=recv_sem.at[turn, side],
                device_id={axis: pos[axis] + step}, device_id_type=MESH,
            )
            pl.when(present)(copy.wait_recv)

    def halo(turn, f, mixed):
        rows = []
        for high in range(2):
            rows.append(jnp.stack([
                jnp.broadcast_to(y_halo[turn, high, f, pl.ds(x, 1), :], (8, 128)) for x in range(8)
            ]))
        columns = []
        for g in range(32):
            k = 32 * f + g
            columns.append(pltpu.roll(mixed, 128 - 2 * k, axis=1) if k else mixed)
        return x_halo[turn, 0, f], x_halo[turn, 1, f], rows[0], rows[1], jnp.stack(columns)

    def mix(turn):
        low = pltpu.roll(z_halo[turn, 0], 1, axis=1)
        high = pltpu.roll(z_halo[turn, 1], 127, axis=1)
        return jnp.where(odd, high, low)

    def around(v):
        zeros4 = jnp.zeros((4, 8, 128), jnp.float32)
        xl = jnp.concatenate([zeros4, v[:28]], axis=0)
        xh = jnp.concatenate([v[4:], zeros4], axis=0)
        zeros1 = jnp.zeros((8, 1, 8, 128), jnp.float32)
        down = pltpu.roll(v, 1, axis=1)
        down4 = down.reshape(8, 4, 8, 128)
        before = jnp.concatenate([zeros1, down4[:, :3]], axis=1).reshape(32, 8, 128)
        yl = jnp.where(sub == 0, before, down)
        up = pltpu.roll(v, 7, axis=1)
        up4 = up.reshape(8, 4, 8, 128)
        after = jnp.concatenate([up4[:, 1:], zeros1], axis=1).reshape(32, 8, 128)
        yh = jnp.where(sub == 7, after, up)
        return xl, xh, yl, yh, pltpu.roll(v, 1, axis=2), pltpu.roll(v, 127, axis=2)

    def interior(v):
        xl, xh, yl, yh, zl, zh = around(v)
        return (
            diag[...] * v - coef_x[0:32] * xl - coef_x[4:36] * xh
            - coef_y[0] * yl - coef_y[1] * yh - coef_z[0] * zl - coef_z[1] * zh
        )

    def border(acc, turn, f, mixed):
        xl, xh, yl, yh, zz = halo(turn, f, mixed)
        acc = acc - edge_z[...] * zz
        acc4 = acc.reshape(8, 4, 8, 128)
        acc = jnp.concatenate([
            (acc4[:, 0] - edge_y[0] * yl)[:, None],
            acc4[:, 1:3],
            (acc4[:, 3] - edge_y[1] * yh)[:, None],
        ], axis=1).reshape(32, 8, 128)
        return jnp.concatenate([
            acc[0:4] - coef_x[0:4] * xl, acc[4:28], acc[28:32] - coef_x[32:36] * xh
        ], axis=0)

    def term(i):
        return basis[i].reshape(32, 8, 128)

    def gram_part(total, pairs):
        for i, j in pairs:
            value = jnp.sum(term(i) * term(j), axis=0)
            value = jnp.sum(value, axis=1, keepdims=True)
            total = jnp.where(lane == SLOT[(i, j)], value, total)
        return total

    basis[0] = dir_ref[...].reshape(256, 128)
    pack(0, [basis.at[0], cond_ref])

    for t in range(groups):
        tile = jnp.zeros((8, 128), jnp.float32)
        for a in range(4):
            amount = ((a - t) * segment) % 128
            rows = gas_ref[8 * a:8 * a + 8, :]
            moved = pltpu.roll(rows, amount, axis=1) if amount else rows
            tile = jnp.where(lane // segment == a, moved, tile)
        flux_send[t] = tile
    pl.semaphore_wait(barrier, count)
    start(0)
    flux_copies = []
    for o in range(1, groups):
        t = lax.rem(pos["gz"] + o, groups)
        flux_copies.append(pltpu.make_async_remote_copy(
            src_ref=flux_send.at[t], dst_ref=flux_halo.at[pos["gz"]],
            send_sem=flux_ssem.at[t], recv_sem=flux_rsem.at[pos["gz"]],
            device_id={"gz": t}, device_id_type=MESH,
        ))
        flux_copies[-1].start()
    flux_halo[pos["gz"]] = flux_send[pos["gz"]]

    xl, xh, yl, yh, zl, zh = around(cond)
    wide = scale[None]
    kx = harmonic(xl, cond) * wide
    coef_x[4:32] = kx[4:32]
    kyl = harmonic(yl, cond) * wide
    kyh = harmonic(yh, cond) * wide
    kzl = jnp.where(lane == 0, 0.0, harmonic(zl, cond) * wide)
    kzh = jnp.where(lane == 127, 0.0, harmonic(zh, cond) * wide)
    coef_y[0] = kyl
    coef_y[1] = kyh
    coef_z[0] = kzl
    coef_z[1] = kzh
    diag_in = (cap - center) * wide + kyl + kyh + kzl + kzh
    total = gram_part(jnp.zeros((8, 128), jnp.float32), [(0, 0)])

    for o in range(1, groups):
        t = lax.rem(pos["gz"] + o, groups)
        pltpu.make_async_remote_copy(
            src_ref=flux_halo.at[t], dst_ref=flux_halo.at[t],
            send_sem=flux_ssem.at[t], recv_sem=flux_rsem.at[t],
            device_id={"gz": t}, device_id_type=MESH,
        ).wait_recv()
    is_top = pos["gx"] == sizes["gx"] - 1
    basis[STEPS + 1] = res_ref[...].reshape(256, 128)
    for a in range(4):
        wanted = map_ref[8 * a:8 * a + 8, :]
        holder = wanted // 128
        index = lax.rem(wanted, 128) + (a - pos["gz"]) * segment
        incoming = jnp.zeros((8, 128), jnp.float32)
        for q in range(groups):
            found = jnp.take_along_axis(flux_halo[q], index, axis=1)
            incoming = jnp.where(holder == q, found, incoming)
        rows = slice(224 + 8 * a, 232 + 8 * a)
        basis[STEPS + 1, rows, :] = res_ref[7, 8 * a:8 * a + 8, :] + jnp.where(is_top, incoming, 0.0)

    wait(0)
    mixed = mix(0)
    xl, xh, yl, yh, zz = halo(0, 1, mixed)
    cond4 = cond.reshape(8, 4, 8, 128)
    coef_x[0:4] = harmonic(xl, cond[0:4]) * wide
    coef_x[32:36] = harmonic(cond[28:32], xh) * wide
    eyl = jnp.where(sub == 0, harmonic(yl, cond4[:, 0]) * wide, 0.0)
    eyh = jnp.where(sub == 7, harmonic(yh, cond4[:, 3]) * wide, 0.0)
    edge_y[0] = eyl
    edge_y[1] = eyh
    ends = jnp.logical_or(lane == 0, lane == 127)
    beside = jnp.where(ends, zz, 0.0)
    ez = harmonic(beside, cond) * wide
    edge_z[...] = ez
    diag_in = diag_in + coef_x[0:32] + coef_x[4:36] + ez
    diag4 = diag_in.reshape(8, 4, 8, 128)
    diag[...] = jnp.concatenate([
        (diag4[:, 0] + eyl)[:, None], diag4[:, 1:3], (diag4[:, 3] + eyh)[:, None]
    ], axis=1).reshape(32, 8, 128)
    basis[1] = (0.5 * border(interior(term(0)), 0, 0, mixed)).reshape(256, 128)

    done = [0]
    for turn in range(1, STEPS):
        d, s = turn, STEPS + turn
        pack(turn, [basis.at[d], basis.at[s]])
        start(turn)
        d_next = interior(term(d))
        s_next = interior(term(s))
        fresh = [d, s]
        done = done + fresh
        total = gram_part(total, [
            (i, j) for i, j in PAIRS if i in done and j in done and (i in fresh or j in fresh)
        ])
        wait(turn)
        mixed = mix(turn)
        d_next = border(d_next, turn, 0, mixed) - term(d - 1)
        s_next = border(s_next, turn, 1, mixed)
        s_next = 0.5 * s_next if turn == 1 else s_next - term(s - 1)
        basis[d + 1] = d_next.reshape(256, 128)
        basis[s + 1] = s_next.reshape(256, 128)

    fresh = [STEPS, 2 * STEPS]
    total = gram_part(total, [(i, j) for i, j in PAIRS if i in fresh or j in fresh])
    row = jnp.sum(total, axis=0, keepdims=True)
    base = 0
    gram_copies = []
    for stage, axes in enumerate(stages):
        members = 1
        for axis in axes:
            members *= sizes[axis]
        own = base + place(axes, pos)
        gram_send[stage] = row
        gram_halo[own] = row
        for peer in peers(axes):
            other = base + place(axes, peer)
            copy = pltpu.make_async_remote_copy(
                src_ref=gram_send.at[stage], dst_ref=gram_halo.at[own],
                send_sem=gram_ssem.at[other], recv_sem=gram_rsem.at[own],
                device_id=peer, device_id_type=MESH,
            )
            copy.start()
            gram_copies.append(copy)
        for peer in peers(axes):
            other = base + place(axes, peer)
            pltpu.make_async_remote_copy(
                src_ref=gram_halo.at[other], dst_ref=gram_halo.at[other],
                send_sem=gram_ssem.at[other], recv_sem=gram_rsem.at[other],
                device_id=peer, device_id_type=MESH,
            ).wait_recv()
        row = jnp.sum(gram_halo[base:base + members], axis=0)
        base += members

    gram = [[None] * DIM for _ in range(DIM)]
    for (i, j), k in SLOT.items():
        gram[i][j] = gram[j][i] = jnp.broadcast_to(row[:, k:k + 1], (8, 128))
    moved, residue, direct = coefficients(gram, center, half_width)

    for weights, out in ((moved, sol_out), (residue, res_out), (direct, dir_out)):
        summed = None
        for i in range(DIM):
            if weights[i] is not None:
                summed = plus(summed, weights[i][None] * term(i))
        if out is sol_out:
            summed = sol_ref[...].reshape(32, 8, 128) + summed
        out[...] = summed.reshape(8, 32, 128)

    for turn in range(STEPS):
        for side, present, copy in copies(turn):
            pl.when(present)(copy.wait_send)
    for copy in flux_copies + gram_copies:
        copy.wait_send()


def solution(mesh):
    sizes = {axis: mesh.shape[axis] for axis in AXES}
    total = sizes["gx"] * sizes["gy"] * sizes["gz"]
    stages = [AXES] if total <= 64 else [(axis,) for axis in AXES]
    rows = 0
    for axes in stages:
        members = 1
        for axis in axes:
            members *= sizes[axis]
        rows += members

    def body(sol, res, direction, material, cond_table, cap_table, gas, supply):
        vmem = pl.BlockSpec(memory_space=pltpu.VMEM)
        smem = pl.BlockSpec(memory_space=pltpu.SMEM)
        f32 = jnp.float32
        block = jax.ShapeDtypeStruct(sol.shape, f32)
        return pl.pallas_call(
            lambda *refs: kernel(sizes, stages, *refs),
            out_shape=(block, block, block),
            in_specs=[smem, smem] + [vmem] * 6,
            out_specs=(vmem, vmem, vmem),
            scratch_shapes=[
                pltpu.VMEM((DIM, 256, 128), f32),
                pltpu.VMEM((36, 8, 128), f32),
                pltpu.VMEM((2, 32, 8, 128), f32),
                pltpu.VMEM((2, 32, 8, 128), f32),
                pltpu.VMEM((2, 8, 8, 128), f32),
                pltpu.VMEM((32, 8, 128), f32),
                pltpu.VMEM((32, 8, 128), f32),
                pltpu.VMEM((256, 128), f32),
                pltpu.VMEM((STEPS, 2, 2, 4, 8, 128), f32),
                pltpu.VMEM((STEPS, 2, 2, 8, 128), f32),
                pltpu.VMEM((STEPS, 8, 128), f32),
                pltpu.VMEM((STEPS, 2, 2, 4, 8, 128), f32),
                pltpu.VMEM((STEPS, 2, 2, 8, 128), f32),
                pltpu.VMEM((STEPS, 2, 8, 128), f32),
                pltpu.VMEM((sizes["gz"], 8, 128), f32),
                pltpu.VMEM((sizes["gz"], 8, 128), f32),
                pltpu.VMEM((len(stages), 1, 128), f32),
                pltpu.VMEM((rows, 1, 128), f32),
                pltpu.SemaphoreType.DMA((STEPS, 6)),
                pltpu.SemaphoreType.DMA((STEPS, 6)),
                pltpu.SemaphoreType.DMA((sizes["gz"],)),
                pltpu.SemaphoreType.DMA((sizes["gz"],)),
                pltpu.SemaphoreType.DMA((rows,)),
                pltpu.SemaphoreType.DMA((rows,)),
            ],
            compiler_params=pltpu.CompilerParams(
                collective_id=0, has_side_effects=True, vmem_limit_bytes=32 * 1024 * 1024
            ),
            cost_estimate=pl.CostEstimate(flops=10**7, bytes_accessed=10**6, transcendentals=0),
        )(cond_table, cap_table, sol, res, direction, material, gas, supply)

    spec = P("gx", "gy", "gz")
    in_specs = (spec, spec, spec, spec, P(), P(), P("gy", "gz"), P("gy", "gz"))
    return jax.shard_map(
        body, mesh=mesh, in_specs=in_specs, out_specs=(spec, spec, spec), check_vma=False
    )
```

```python
import jax
import jax.numpy as jnp
from jax import lax
from jax.experimental import pallas as pl
from jax.experimental.pallas import tpu as pltpu
from jax.sharding import PartitionSpec as P

STEPS = 4
VMEM = 63 * 1024 * 1024
AXES = ("gx", "gy", "gz")
MESH = pl.DeviceIdType.MESH
DIM = 2 * STEPS + 1
PAIRS = [(i, j) for i in range(DIM) for j in range(i, DIM)]
SLOT = {pair: k for k, pair in enumerate(PAIRS)}


def harmonic(a, b):
    return 2.0 * a * b / (a + b)


def tree(parts):
    while len(parts) > 1:
        parts = [sum(parts[k:k + 2][1:], parts[k]) for k in range(0, len(parts), 2)]
    return parts[0]


def times(a, b):
    return None if a is None or b is None else a * b


def plus(a, b):
    return b if a is None else a if b is None else a + b


def shift_product(p, center, half_width):
    q = [None] * DIM
    for offset, length in ((0, STEPS + 1), (STEPS + 1, STEPS)):
        for column in range(length - 1):
            entry = p[offset + column]
            if entry is None:
                continue
            q[offset + column] = plus(q[offset + column], center * entry)
            low = half_width if column == 0 else 0.5 * half_width
            q[offset + column + 1] = plus(q[offset + column + 1], low * entry)
            if column >= 1:
                q[offset + column - 1] = plus(q[offset + column - 1], 0.5 * half_width * entry)
    return q


def form(gram, a, b):
    total = None
    for i in range(DIM):
        if a[i] is None:
            continue
        row = None
        for j in range(DIM):
            row = plus(row, times(gram[i][j], b[j]))
        total = plus(total, a[i] * row)
    return total


def coefficients(gram, center, half_width):
    one = jnp.ones_like(gram[0][0])
    p = [None] * DIM
    r = [None] * DIM
    x = [None] * DIM
    p[0] = one
    r[STEPS + 1] = one
    rr = form(gram, r, r)
    for _ in range(STEPS):
        q = shift_product(p, center, half_width)
        step = rr / form(gram, p, q)
        x = [plus(x[i], times(step, p[i])) for i in range(DIM)]
        r = [plus(r[i], times(-step, q[i])) for i in range(DIM)]
        new = form(gram, r, r)
        ratio = new / rr
        p = [plus(r[i], times(ratio, p[i])) for i in range(DIM)]
        rr = new
    return x, r, p


def kernel(
    sizes, stages, cond_in, cap_in, sol_in, res_in, dir_in, mat_in, gas_in, map_in,
    sol_out, res_out, dir_out,
    basis, held, store_sem, cond_tab, cap_tab, res_ref, mat_ref, gas_ref, map_ref,
    coef_x, coef_y, coef_z, edge_y, edge_z, diag, cond_ref,
    x_send, y_send, z_send, x_halo, y_halo, z_halo, flux_send, flux_halo, gram_send, gram_halo,
    send_sem, recv_sem, flux_ssem, flux_rsem, gram_ssem, gram_rsem, load_sem,
):
    loads = []
    for source, target in (
        (dir_in, basis.at[0]), (mat_in, mat_ref), (cond_in, cond_tab), (cap_in, cap_tab),
        (gas_in, gas_ref), (res_in, res_ref), (map_in, map_ref), (sol_in, held.at[0]),
    ):
        loads.append(pltpu.make_async_copy(source, target, load_sem.at[len(loads)]))
    pos = {axis: lax.axis_index(axis) for axis in AXES}
    groups = sizes["gz"]
    segment = 128 // groups
    lane = lax.broadcasted_iota(jnp.int32, (8, 128), 1)
    sub = lax.broadcasted_iota(jnp.int32, (8, 128), 0)

    sides = []
    for number, axis in enumerate(AXES):
        if sizes[axis] > 1:
            sides.append((2 * number, axis, -1, pos[axis] > 0))
            sides.append((2 * number + 1, axis, 1, pos[axis] < sizes[axis] - 1))

    def zero(side):
        number, high = side // 2, side % 2
        ref = (x_halo, y_halo, z_halo)[number]
        ref[:, high] = jnp.zeros(ref.shape[:1] + ref.shape[2:], jnp.float32)

    for side in range(6):
        present = [entry[3] for entry in sides if entry[0] == side]
        if present:
            pl.when(jnp.logical_not(present[0]))(lambda side=side: zero(side))
        else:
            zero(side)

    def peers(axes):
        found = [{}]
        for axis in axes:
            found = [dict(entry, **{axis: o}) for entry in found for o in range(sizes[axis])]
        found = [entry for entry in found if any(entry.values())]
        return [
            {axis: lax.rem(pos[axis] + o, sizes[axis]) for axis, o in entry.items()} for entry in found
        ]

    def place(axes, where):
        index = 0
        for axis in axes:
            index = index * sizes[axis] + where[axis]
        return index

    barrier = pltpu.get_barrier_semaphore()
    count = 0
    for axis in AXES:
        for peer in peers((axis,)):
            pl.semaphore_signal(barrier, inc=1, device_id=peer, device_id_type=MESH)
            count += 1
    for load in loads:
        load.start()
    for load in loads[:4]:
        load.wait()

    material = mat_ref[...]
    cond = jnp.full((32, 8, 128), cond_tab[0], jnp.float32)
    cap = jnp.full((32, 8, 128), cap_tab[0], jnp.float32)
    cond_max = cond_tab[0]
    cap_max = cap_tab[0]
    cap_min = cap_tab[0]
    for m in range(1, 8):
        hit = material == m
        cond = jnp.where(hit, cond_tab[m], cond)
        cap = jnp.where(hit, cap_tab[m], cap)
        cond_max = jnp.maximum(cond_max, cond_tab[m])
        cap_max = jnp.maximum(cap_max, cap_tab[m])
        cap_min = jnp.minimum(cap_min, cap_tab[m])
    highest = cap_max + 12.0 * cond_max
    center = jnp.full((8, 128), 0.5 * (highest + cap_min), jnp.float32)
    half_width = jnp.full((8, 128), 0.5 * (highest - cap_min), jnp.float32)
    cond_ref[...] = cond.reshape(256, 128)

    odd = lax.rem(lane, 2) == 1
    pair_of = lax.rem(lane + 1, 128) // 2

    def copies(turn):
        result = []
        for side, axis, step, present in sides:
            number, high = side // 2, side % 2
            source = (x_send.at[turn, high], y_send.at[turn, high], z_send.at[turn])[number]
            target = (x_halo, y_halo, z_halo)[number].at[turn, 1 - high]
            result.append((side, present, pltpu.make_async_remote_copy(
                src_ref=source, dst_ref=target,
                send_sem=send_sem.at[turn, side], recv_sem=recv_sem.at[turn, side ^ 1],
                device_id={axis: pos[axis] + step}, device_id_type=MESH,
            )))
        return result

    def pack(turn, refs):
        tile = jnp.zeros((8, 128), jnp.float32)
        for f, ref in enumerate(refs):
            value = ref[...].reshape(32, 8, 128)
            x_send[turn, 0, f] = value[0:4]
            x_send[turn, 1, f] = value[28:32]
            y_send[turn, 0, f] = ref[pl.ds(0, 8, stride=32), :]
            y_send[turn, 1, f] = ref[pl.ds(31, 8, stride=32), :]
            for g in range(32):
                k = 32 * f + g
                moved = pltpu.roll(value[g], 2 * k, axis=1) if k else value[g]
                tile = jnp.where(pair_of == k, moved, tile)
        z_send[turn] = tile

    def start(turn):
        for side, present, copy in copies(turn):
            pl.when(present)(copy.start)

    def wait(turn):
        for side, axis, step, present in sides:
            number, high = side // 2, side % 2
            target = (x_halo, y_halo, z_halo)[number].at[turn, high]
            copy = pltpu.make_async_remote_copy(
                src_ref=target, dst_ref=target,
                send_sem=send_sem.at[turn, side], recv_sem=recv_sem.at[turn, side],
                device_id={axis: pos[axis] + step}, device_id_type=MESH,
            )
            pl.when(present)(copy.wait_recv)

    def halo(turn, f, mixed):
        rows = []
        for high in range(2):
            rows.append(jnp.stack([
                jnp.broadcast_to(y_halo[turn, high, f, pl.ds(x, 1), :], (8, 128)) for x in range(8)
            ]))
        columns = []
        for g in range(32):
            k = 32 * f + g
            columns.append(pltpu.roll(mixed, 128 - 2 * k, axis=1) if k else mixed)
        return x_halo[turn, 0, f], x_halo[turn, 1, f], rows[0], rows[1], jnp.stack(columns)

    def mix(turn):
        low = pltpu.roll(z_halo[turn, 0], 1, axis=1)
        high = pltpu.roll(z_halo[turn, 1], 127, axis=1)
        return jnp.where(odd, high, low)

    def around(v):
        zeros4 = jnp.zeros((4, 8, 128), jnp.float32)
        xl = jnp.concatenate([zeros4, v[:28]], axis=0)
        xh = jnp.concatenate([v[4:], zeros4], axis=0)
        zeros1 = jnp.zeros((8, 1, 8, 128), jnp.float32)
        down = pltpu.roll(v, 1, axis=1)
        down4 = down.reshape(8, 4, 8, 128)
        before = jnp.concatenate([zeros1, down4[:, :3]], axis=1).reshape(32, 8, 128)
        yl = jnp.where(sub == 0, before, down)
        up = pltpu.roll(v, 7, axis=1)
        up4 = up.reshape(8, 4, 8, 128)
        after = jnp.concatenate([up4[:, 1:], zeros1], axis=1).reshape(32, 8, 128)
        yh = jnp.where(sub == 7, after, up)
        return xl, xh, yl, yh, pltpu.roll(v, 1, axis=2), pltpu.roll(v, 127, axis=2)

    def interior(v):
        xl, xh, yl, yh, zl, zh = around(v)
        return (
            diag[...] * v - coef_x[0:32] * xl - coef_x[4:36] * xh
            - coef_y[0] * yl - coef_y[1] * yh - coef_z[0] * zl - coef_z[1] * zh
        )

    def border(acc, turn, f, mixed):
        xl, xh, yl, yh, zz = halo(turn, f, mixed)
        acc = acc - edge_z[...] * zz
        acc4 = acc.reshape(8, 4, 8, 128)
        acc = jnp.concatenate([
            (acc4[:, 0] - edge_y[0] * yl)[:, None],
            acc4[:, 1:3],
            (acc4[:, 3] - edge_y[1] * yh)[:, None],
        ], axis=1).reshape(32, 8, 128)
        return jnp.concatenate([
            acc[0:4] - coef_x[0:4] * xl, acc[4:28], acc[28:32] - coef_x[32:36] * xh
        ], axis=0)

    def term(i):
        return basis[i].reshape(32, 8, 128)

    def gram_part(total, pairs):
        for i, j in pairs:
            product = term(i) * term(j)
            value = tree([tree([product[8 * a + g] for a in range(4)]) for g in range(8)])
            value = jnp.sum(value, axis=1, keepdims=True)
            total = jnp.where(lane == SLOT[(i, j)], value, total)
        return total

    pack(0, [basis.at[0], cond_ref])

    loads[4].wait()
    for t in range(groups):
        tile = jnp.zeros((8, 128), jnp.float32)
        for a in range(4):
            amount = ((a - t) * segment) % 128
            rows = gas_ref[8 * a:8 * a + 8, :]
            moved = pltpu.roll(rows, amount, axis=1) if amount else rows
            tile = jnp.where(lane // segment == a, moved, tile)
        flux_send[t] = tile
    pl.semaphore_wait(barrier, count)
    start(0)
    flux_copies = []
    for o in range(1, groups):
        t = lax.rem(pos["gz"] + o, groups)
        flux_copies.append(pltpu.make_async_remote_copy(
            src_ref=flux_send.at[t], dst_ref=flux_halo.at[pos["gz"]],
            send_sem=flux_ssem.at[t], recv_sem=flux_rsem.at[pos["gz"]],
            device_id={"gz": t}, device_id_type=MESH,
        ))
        flux_copies[-1].start()
    flux_halo[pos["gz"]] = flux_send[pos["gz"]]

    xl, xh, yl, yh, zl, zh = around(cond)
    kx = harmonic(xl, cond)
    coef_x[4:32] = kx[4:32]
    kyl = harmonic(yl, cond)
    kyh = harmonic(yh, cond)
    kzl = jnp.where(lane == 0, 0.0, harmonic(zl, cond))
    kzh = jnp.where(lane == 127, 0.0, harmonic(zh, cond))
    coef_y[0] = kyl
    coef_y[1] = kyh
    coef_z[0] = kzl
    coef_z[1] = kzh
    diag_in = (cap - center) + kyl + kyh + kzl + kzh
    total = gram_part(jnp.zeros((8, 128), jnp.float32), [(0, 0)])

    for o in range(1, groups):
        t = lax.rem(pos["gz"] + o, groups)
        pltpu.make_async_remote_copy(
            src_ref=flux_halo.at[t], dst_ref=flux_halo.at[t],
            send_sem=flux_ssem.at[t], recv_sem=flux_rsem.at[t],
            device_id={"gz": t}, device_id_type=MESH,
        ).wait_recv()
    is_top = pos["gx"] == sizes["gx"] - 1
    loads[5].wait()
    loads[6].wait()
    basis[STEPS + 1] = res_ref[...]
    for a in range(4):
        wanted = map_ref[8 * a:8 * a + 8, :]
        holder = wanted // 128
        index = lax.rem(wanted, 128) + (a - pos["gz"]) * segment
        incoming = jnp.zeros((8, 128), jnp.float32)
        for q in range(groups):
            found = jnp.take_along_axis(flux_halo[q], index, axis=1)
            incoming = jnp.where(holder == q, found, incoming)
        rows = slice(224 + 8 * a, 232 + 8 * a)
        basis[STEPS + 1, rows, :] = res_ref[rows, :] + jnp.where(is_top, incoming, 0.0)

    wait(0)
    mixed = mix(0)
    xl, xh, yl, yh, zz = halo(0, 1, mixed)
    cond4 = cond.reshape(8, 4, 8, 128)
    coef_x[0:4] = harmonic(xl, cond[0:4])
    coef_x[32:36] = harmonic(cond[28:32], xh)
    eyl = jnp.where(sub == 0, harmonic(yl, cond4[:, 0]), 0.0)
    eyh = jnp.where(sub == 7, harmonic(yh, cond4[:, 3]), 0.0)
    edge_y[0] = eyl
    edge_y[1] = eyh
    ends = jnp.logical_or(lane == 0, lane == 127)
    beside = jnp.where(ends, zz, 0.0)
    ez = harmonic(beside, cond)
    edge_z[...] = ez
    diag_in = diag_in + coef_x[0:32] + coef_x[4:36] + ez
    diag4 = diag_in.reshape(8, 4, 8, 128)
    diag[...] = jnp.concatenate([
        (diag4[:, 0] + eyl)[:, None], diag4[:, 1:3], (diag4[:, 3] + eyh)[:, None]
    ], axis=1).reshape(32, 8, 128)
    basis[1] = (border(interior(term(0)), 0, 0, mixed) / half_width).reshape(256, 128)

    done = [0]
    for turn in range(1, STEPS):
        d, s = turn, STEPS + turn
        pack(turn, [basis.at[d], basis.at[s]])
        start(turn)
        d_next = interior(term(d))
        s_next = interior(term(s))
        fresh = [d, s]
        done = done + fresh
        total = gram_part(total, [
            (i, j) for i, j in PAIRS if i in done and j in done and (i in fresh or j in fresh)
        ])
        wait(turn)
        mixed = mix(turn)
        d_next = 2.0 * (border(d_next, turn, 0, mixed) / half_width) - term(d - 1)
        s_next = border(s_next, turn, 1, mixed) / half_width
        s_next = s_next if turn == 1 else 2.0 * s_next - term(s - 1)
        basis[d + 1] = d_next.reshape(256, 128)
        basis[s + 1] = s_next.reshape(256, 128)

    fresh = [STEPS, 2 * STEPS]
    total = gram_part(total, [(i, j) for i, j in PAIRS if i in fresh or j in fresh])
    row = jnp.sum(total, axis=0, keepdims=True)
    base = 0
    gram_copies = []
    for stage, axes in enumerate(stages):
        members = 1
        for axis in axes:
            members *= sizes[axis]
        own = base + place(axes, pos)
        gram_send[stage] = row
        gram_halo[own] = row
        for peer in peers(axes):
            other = base + place(axes, peer)
            copy = pltpu.make_async_remote_copy(
                src_ref=gram_send.at[stage], dst_ref=gram_halo.at[own],
                send_sem=gram_ssem.at[other], recv_sem=gram_rsem.at[own],
                device_id=peer, device_id_type=MESH,
            )
            copy.start()
            gram_copies.append(copy)
        for peer in peers(axes):
            other = base + place(axes, peer)
            pltpu.make_async_remote_copy(
                src_ref=gram_halo.at[other], dst_ref=gram_halo.at[other],
                send_sem=gram_ssem.at[other], recv_sem=gram_rsem.at[other],
                device_id=peer, device_id_type=MESH,
            ).wait_recv()
        row = tree([gram_halo[base + member] for member in range(members)])
        base += members

    gram = [[None] * DIM for _ in range(DIM)]
    for (i, j), k in SLOT.items():
        gram[i][j] = gram[j][i] = jnp.broadcast_to(row[:, k:k + 1], (8, 128))
    moved, residue, direct = coefficients(gram, center, half_width)

    stores = []
    loads[7].wait()
    for number, weights, out in ((1, residue, res_out), (2, direct, dir_out), (0, moved, sol_out)):
        summed = held[0] if number == 0 else None
        for i in range(DIM):
            if weights[i] is not None:
                summed = plus(summed, weights[i][None] * term(i))
        held[number] = summed
        stores.append(pltpu.make_async_copy(held.at[number], out, store_sem.at[number]))
        stores[-1].start()

    for turn in range(STEPS):
        for side, present, copy in copies(turn):
            pl.when(present)(copy.wait_send)
    for copy in flux_copies + gram_copies:
        copy.wait_send()
    for store in stores:
        store.wait()


def finish(res_in, dir_in, sol_in, res_out, dir_out, sol_out, held, load_sem, store_sem):
    loads = []
    for source in (res_in, dir_in, sol_in):
        k = len(loads)
        loads.append(pltpu.make_async_copy(source, held.at[k], load_sem.at[k]))
        loads[k].start()
    stores = []
    for target in (res_out, dir_out, sol_out):
        k = len(stores)
        loads[k].wait()
        stores.append(pltpu.make_async_copy(held.at[k], target, store_sem.at[k]))
        stores[k].start()
    for store in stores:
        store.wait()


def solution(mesh):
    sizes = {axis: mesh.shape[axis] for axis in AXES}
    total = sizes["gx"] * sizes["gy"] * sizes["gz"]
    stages = [AXES] if total <= 64 else [(axis,) for axis in AXES]
    rows = 0
    for axes in stages:
        members = 1
        for axis in axes:
            members *= sizes[axis]
        rows += members

    def body(sol, res, direction, material, cond_table, cap_table, gas, supply):
        hbm = pl.BlockSpec(memory_space=pltpu.HBM)
        f32 = jnp.float32
        block = jax.ShapeDtypeStruct((32, 8, 128), f32)
        flat = [value.reshape(256, 128) for value in (res, direction)]
        fields = pl.pallas_call(
            lambda *refs: kernel(sizes, stages, *refs),
            out_shape=(block, block, block),
            in_specs=[hbm] * 8,
            out_specs=(hbm, hbm, hbm),
            scratch_shapes=[
                pltpu.VMEM((DIM, 256, 128), f32),
                pltpu.VMEM((3, 32, 8, 128), f32),
                pltpu.SemaphoreType.DMA((3,)),
                pltpu.SMEM((8,), f32),
                pltpu.SMEM((8,), f32),
                pltpu.VMEM((256, 128), f32),
                pltpu.VMEM((32, 8, 128), jnp.int32),
                pltpu.VMEM((32, 128), f32),
                pltpu.VMEM((32, 128), jnp.int32),
                pltpu.VMEM((36, 8, 128), f32),
                pltpu.VMEM((2, 32, 8, 128), f32),
                pltpu.VMEM((2, 32, 8, 128), f32),
                pltpu.VMEM((2, 8, 8, 128), f32),
                pltpu.VMEM((32, 8, 128), f32),
                pltpu.VMEM((32, 8, 128), f32),
                pltpu.VMEM((256, 128), f32),
                pltpu.VMEM((STEPS, 2, 2, 4, 8, 128), f32),
                pltpu.VMEM((STEPS, 2, 2, 8, 128), f32),
                pltpu.VMEM((STEPS, 8, 128), f32),
                pltpu.VMEM((STEPS, 2, 2, 4, 8, 128), f32),
                pltpu.VMEM((STEPS, 2, 2, 8, 128), f32),
                pltpu.VMEM((STEPS, 2, 8, 128), f32),
                pltpu.VMEM((sizes["gz"], 8, 128), f32),
                pltpu.VMEM((sizes["gz"], 8, 128), f32),
                pltpu.VMEM((len(stages), 1, 128), f32),
                pltpu.VMEM((rows, 1, 128), f32),
                pltpu.SemaphoreType.DMA((STEPS, 6)),
                pltpu.SemaphoreType.DMA((STEPS, 6)),
                pltpu.SemaphoreType.DMA((sizes["gz"],)),
                pltpu.SemaphoreType.DMA((sizes["gz"],)),
                pltpu.SemaphoreType.DMA((rows,)),
                pltpu.SemaphoreType.DMA((rows,)),
                pltpu.SemaphoreType.DMA((8,)),
            ],
            compiler_params=pltpu.CompilerParams(
                collective_id=0, has_side_effects=True, vmem_limit_bytes=VMEM
            ),
            cost_estimate=pl.CostEstimate(flops=10**7, bytes_accessed=10**6, transcendentals=0),
        )(cond_table, cap_table, sol.reshape(32, 8, 128), *flat, material.reshape(32, 8, 128), gas, supply)
        outs = pl.pallas_call(
            finish,
            out_shape=(block, block, block),
            in_specs=[hbm] * 3,
            out_specs=(hbm, hbm, hbm),
            scratch_shapes=[
                pltpu.VMEM((3, 32, 8, 128), f32),
                pltpu.SemaphoreType.DMA((3,)),
                pltpu.SemaphoreType.DMA((3,)),
            ],
            compiler_params=pltpu.CompilerParams(vmem_limit_bytes=VMEM),
        )(fields[1], fields[2], fields[0])
        return tuple(value.reshape(sol.shape) for value in (outs[2], outs[0], outs[1]))

    spec = P("gx", "gy", "gz")
    in_specs = (spec, spec, spec, spec, P(), P(), P("gy", "gz"), P("gy", "gz"))
    return jax.shard_map(
        body, mesh=mesh, in_specs=in_specs, out_specs=(spec, spec, spec), check_vma=False
    )
```
